32 devices in a mesh: lat: 4 (over y, x), lon: 8 (over z, core).
Axes of the slice: x: 2, y: 2, z: 4, core: 2. Of those that a mesh axis runs over, the one named last changes fastest.
Arguments:
- tokens: bfloat16 [32, 128, 1024], P('lat', 'lon'), may hold values from -60 to 60
- norm1_gain: float32 [1024], replicated, may hold values from 0.5 to 1.5
- conv_weight: float32 [3, 3, 1024], replicated, may hold values from -1.5 to 1.5
- norm2_gain: float32 [1024], replicated, may hold values from 0.5 to 1.5
- w_query: bfloat16 [1024, 1024], replicated, may hold values from -1 to 1
- w_key: bfloat16 [1024, 1024], replicated, may hold values from -1 to 1
- w_value: bfloat16 [1024, 1024], replicated, may hold values from -0.1875 to 0.1875
- w_out: bfloat16 [1024, 1024], replicated, may hold values from -0.1875 to 0.1875
- head_scale: float32 [16], replicated, may hold values from 4 to 32
- pattern: int32 [4, 8, 8], P('lat', 'lon'), may hold values from 0 to 31, as said below
Outputs:
- result: bfloat16 [32, 128, 1024], P('lat', 'lon')
The draws below stay inside these ranges and needn't reach their ends.
Inputs may be any that keep to these rules, and one draw needn't show every extreme that they name: `pattern`: each row lists 8 different tiles; the first is the query tile itself; every listed tile lies in the query's band or a neighbouring band, in the query's longitude sector (the tiles of one device along `lon`) or one of the two sectors beside it around the globe; every query tile of the first and last band also lists both tiles of its own band two sectors away on either side around the globe; query tiles of other bands never list such tiles.
All inputs are finite; a program needn't handle non-finite values.
Results may differ from the reference program's by a relative error of at most 0.018.
Values may be sent and summed in bfloat16 or wider, within the bound.
No kernel may reach another device: no remote copies, remote signals or barrier semaphores. Data moves between devices by JAX's collectives and lax.ppermute only.
A program may use at most 64 MiB of HBM per device.

```python
import math
import jax
import jax.numpy as jnp
from jax import lax

D = 1024
H = 16
HD = 64
TILE_LAT = 8
TILE_LON = 16
KEY_TILES = 8
TILES_DEV = 1
NLAT = 32
NLON = 128
TLON = 8
N_LAT = 4
N_LON = 8


def draw_tokens(key, part):
    rough = jax.random.normal(jax.random.fold_in(key, 21), (NLAT, NLON, D), jnp.float32)
    drawn = rough
    return jnp.clip(drawn, -60.0, 60.0).astype(jnp.bfloat16)


def projection_pair(key):
    base = jax.random.normal(jax.random.fold_in(key, 41), (D, D), jnp.float32) / math.sqrt(D)
    other = jax.random.normal(jax.random.fold_in(key, 42), (D, D), jnp.float32) / math.sqrt(D)
    paired = other
    return (jnp.clip(base, -1.0, 1.0), jnp.clip(paired, -1.0, 1.0))


def draw_w_query(key, part):
    return projection_pair(key)[0].astype(jnp.bfloat16)


def draw_w_key(key, part):
    return projection_pair(key)[1].astype(jnp.bfloat16)


def draw_pattern(key, part):
    tile_cols = TILES_DEV * N_LON
    cand_count = 11 * TILES_DEV
    band_ids = jnp.arange(N_LAT, dtype=jnp.int32)[:, None, None]
    column = jnp.arange(tile_cols, dtype=jnp.int32)[None, :, None]
    slot_ids = jnp.arange(cand_count, dtype=jnp.int32)[None, None, :]
    sector = column // TILES_DEV
    within = column % TILES_DEV
    near_slot = slot_ids < 9 * TILES_DEV
    slot_group = slot_ids // TILES_DEV
    tile_pos = slot_ids % TILES_DEV
    band_off = jnp.where(near_slot, slot_group // 3 - 1, 0)
    sector_off = jnp.where(near_slot, slot_group % 3 - 1, jnp.where(slot_group == 9, -2, 2))
    key_band = band_ids + band_off
    key_sector = (sector + sector_off) % N_LON
    key_tile = key_band * tile_cols + key_sector * TILES_DEV + tile_pos
    polar_band = (band_ids == 0) | (band_ids == N_LAT - 1)
    usable = (key_band >= 0) & (key_band < N_LAT) & (near_slot | polar_band)
    is_self = (band_off == 0) & (sector_off == 0) & (tile_pos == within)
    draw_shape = (N_LAT, tile_cols, 1)
    pick_sign = jax.random.randint(jax.random.fold_in(key, 31), draw_shape, 0, 2)
    pick_sector = jax.random.randint(jax.random.fold_in(key, 32), draw_shape, -1, 2)
    pick_tile = jax.random.randint(jax.random.fold_in(key, 33), draw_shape, 0, TILES_DEV)
    far_sign = 2 * pick_sign - 1
    want_band = jnp.where(polar_band, 0, far_sign)
    want_sector = jnp.where(polar_band, 2 * far_sign, pick_sector)
    forced = (band_off == want_band) & (sector_off == want_sector) & (tile_pos == pick_tile)
    draw_noise = jax.random.randint(jax.random.fold_in(key, 34), (N_LAT, tile_cols, cand_count), 0, 65536)
    ranking = jnp.where(usable, draw_noise * cand_count + slot_ids, -1 - slot_ids)
    ranking = jnp.where(forced, 2 ** 27 + slot_ids, ranking)
    ranking = jnp.where(is_self, 2 ** 28, ranking)
    best_scores, chosen = lax.top_k(ranking, KEY_TILES)
    all_tiles = jnp.broadcast_to(key_tile, ranking.shape)
    return jnp.take_along_axis(all_tiles, chosen, axis=2).astype(jnp.int32)


def gaussian(stream_key, extent, deviation, most, held_as=jnp.bfloat16):
    values = jax.random.normal(stream_key, extent, jnp.float32) * deviation
    return jnp.minimum(jnp.maximum(values, -most), most).astype(held_as)


def setup_inputs(seed: int = 0) -> dict:
    keys = jax.random.split(jax.random.key(seed), 11)
    return {
        "tokens": draw_tokens(jax.random.fold_in(keys[10], 71), 0),
        "norm1_gain": jnp.clip(1.0 + 0.1 * jax.random.normal(keys[1], (D,), jnp.float32), 0.5, 1.5),
        "conv_weight": gaussian(keys[2], (3, 3, D), 0.25, 1.5, jnp.float32),
        "norm2_gain": jnp.clip(1.0 + 0.1 * jax.random.normal(keys[3], (D,), jnp.float32), 0.5, 1.5),
        "w_query": draw_w_query(jax.random.fold_in(keys[10], 71), 0),
        "w_key": draw_w_key(jax.random.fold_in(keys[10], 71), 0),
        "w_value": gaussian(keys[6], (D, D), D ** -0.5, 0.1875),
        "w_out": gaussian(keys[7], (D, D), D ** -0.5, 0.1875),
        "head_scale": jnp.clip(jnp.exp(jax.random.uniform(keys[8], (H,), jnp.float32, math.log(4.0), math.log(32.0))), 4.0, 32.0),
        "pattern": draw_pattern(jax.random.fold_in(keys[10], 71), 0),
    }


def rms_norm(values, gain):
    widened = values.astype(jnp.float32)
    return widened * lax.rsqrt(lax.optimization_barrier(jnp.mean(widened * widened, axis=-1, keepdims=True)) + 1e-06) * gain

def head_norm(values):
    return values * lax.rsqrt(lax.optimization_barrier(jnp.mean(values * values, axis=-1, keepdims=True)) + 1e-06)

def to_tiles(grid):
    extra = grid.shape[2:]
    shaped = grid.reshape((N_LAT, TILE_LAT, TLON, TILE_LON) + extra)
    moved = jnp.moveaxis(shaped, 2, 1)
    return moved.reshape((N_LAT * TLON, TILE_LAT * TILE_LON) + extra)

def from_tiles(tiled):
    extra = tiled.shape[2:]
    shaped = tiled.reshape((N_LAT, TLON, TILE_LAT, TILE_LON) + extra)
    moved = jnp.moveaxis(shaped, 2, 1)
    return moved.reshape((NLAT, NLON) + extra)

def reference(tokens, norm1_gain, conv_weight, norm2_gain, w_query, w_key, w_value, w_out, head_scale, pattern):
    normed = rms_norm(tokens, norm1_gain).astype(jnp.bfloat16)
    normed = lax.optimization_barrier(normed).astype(jnp.float32)
    padded = jnp.pad(normed, ((1, 1), (0, 0), (0, 0)))
    padded = jnp.concatenate([padded[:, -1:], padded, padded[:, :1]], axis=1)
    conv_sum = jnp.zeros(tokens.shape, jnp.float32)
    for row_off in range(3):
        for col_off in range(3):
            conv_sum = conv_sum + padded[row_off:row_off + NLAT, col_off:col_off + NLON] * conv_weight[row_off, col_off]
    hidden = (tokens.astype(jnp.float32) + conv_sum).astype(jnp.bfloat16)
    second = rms_norm(hidden, norm2_gain).astype(jnp.bfloat16).reshape(NLAT * NLON, D)
    queries = head_norm(jnp.dot(second, w_query, preferred_element_type=jnp.float32).reshape(-1, H, HD)).astype(jnp.bfloat16)
    keys_all = head_norm(jnp.dot(second, w_key, preferred_element_type=jnp.float32).reshape(-1, H, HD)).astype(jnp.bfloat16)
    values_all = jnp.dot(second, w_value, preferred_element_type=jnp.float32).astype(jnp.bfloat16).reshape(-1, H, HD)
    query_tiles = to_tiles(queries.reshape(NLAT, NLON, H, HD))
    key_tiles = to_tiles(keys_all.reshape(NLAT, NLON, H, HD))
    value_tiles = to_tiles(values_all.reshape(NLAT, NLON, H, HD))
    factor = head_scale * (1.0 / math.sqrt(HD))
    span = KEY_TILES * TILE_LAT * TILE_LON

    def one_tile(item):
        own, tile_ids = item
        keys_sel = jnp.take(key_tiles, tile_ids, axis=0).reshape(span, H, HD)
        values_sel = jnp.take(value_tiles, tile_ids, axis=0).reshape(span, H, HD)
        scores = jnp.einsum('qhe,khe->hqk', own.astype(jnp.float32), keys_sel.astype(jnp.float32)) * factor[:, None, None]
        row_max = lax.optimization_barrier(jnp.max(scores, axis=-1, keepdims=True))
        exponent = jnp.exp(scores - row_max)
        attn_weights = (exponent / lax.optimization_barrier(jnp.sum(exponent, axis=-1, keepdims=True))).astype(jnp.bfloat16)
        mixed = jnp.einsum('hqk,khe->qhe', attn_weights.astype(jnp.float32), values_sel.astype(jnp.float32))
        return mixed.astype(jnp.bfloat16)
    attended = lax.map(one_tile, (query_tiles, pattern.reshape(-1, KEY_TILES)))
    attended_grid = from_tiles(attended).reshape(NLAT * NLON, D)
    result = hidden.astype(jnp.float32).reshape(NLAT * NLON, D) + jnp.dot(attended_grid, w_out, preferred_element_type=jnp.float32)
    return result.astype(jnp.bfloat16).reshape(NLAT, NLON, D)
```

```python
import functools
import math

import jax
import jax.numpy as jnp
from jax import lax
from jax.experimental import pallas as pl
from jax.experimental.pallas import tpu as pltpu
from jax.sharding import PartitionSpec as P

EPS = 1e-06
HALO = 7
BIG = 1e30
VMEM = pl.BlockSpec(memory_space=pltpu.VMEM)
SMEM = pl.BlockSpec(memory_space=pltpu.SMEM)


def pair_swaps(count, first):
    pairs = []
    for low in range(first, count - 1, 2):
        pairs += [(low, low + 1), (low + 1, low)]
    return pairs


def lon_pairs(lats, lat_count, lon_count, off_chip):
    pairs = []
    for lat in lats:
        for low in range(1 if off_chip else 0, lon_count, 2):
            one, two = lat * lon_count + low, lat * lon_count + (low + 1) % lon_count
            pairs += [(one, two), (two, one)]
    return pairs


def two_away(count, first):
    pairs = []
    for start in range(first, count, 4):
        for low in (start, start + 1):
            if low + 2 < count:
                pairs += [(low, low + 2), (low + 2, low)]
    return pairs


def permuted(value, axis, pairs):
    if not pairs:
        return jnp.zeros_like(value)
    return lax.ppermute(value, axis, pairs)


def unit(values):
    return lax.rsqrt(jnp.mean(values * values, axis=-1, keepdims=True) + EPS)


def conv_kernel(
    meta, tok, tile_a, tile_b, halo, halo_a, halo_b, ring_a, ring_b, gain1, weight, gain2,
    hidden, second, second_a, second_b, window,
):
    rows, cols, width = tok.shape
    left, main = HALO, slice(HALO + 1, HALO + 1 + cols)
    right = HALO + 1 + cols
    gain_one, gain_two = gain1[...], gain2[...]

    def normed(raw):
        wide = raw.astype(jnp.float32)
        gain = gain_one if wide.ndim == 2 else gain_one[None]
        return (wide * unit(wide) * gain).astype(jnp.bfloat16).astype(jnp.float32)

    def place(base, raw, edges):
        for row in range(rows):
            window[base + row, main, :] = normed(raw[row])
        sides = normed(edges[...])
        for row in range(rows):
            window[base + row, left : left + 1, :] = sides[row : row + 1]
            window[base + row, right : right + 1, :] = sides[rows + row : rows + row + 1]

    def ring(row, data, bottom):
        base = pl.multiple_of(bottom * cols, cols)
        window[row, main, :] = normed(data[pl.ds(base, cols), :])
        sides = normed(data[2 * cols :, :])
        first, last = sides[0:1], sides[rows - 1 : rows]
        window[row, left : left + 1, :] = jnp.where(bottom > 0, last, first)
        first, last = sides[rows : rows + 1], sides[2 * rows - 1 : 2 * rows]
        window[row, right : right + 1, :] = jnp.where(bottom > 0, last, first)

    odd, high = meta[10], meta[11]
    base_own = 1 + rows
    base_a = jnp.where(odd > 0, 1, 1 + 2 * rows)
    base_b = jnp.where(odd > 0, 1 + 2 * rows, 1)
    last_row = 1 + 3 * rows
    place(base_own, tok, halo)
    place(base_a, tile_a, halo_a)
    place(base_b, tile_b, halo_b)
    ring(jnp.where(high > 0, 0, last_row), ring_a, high)
    ring(jnp.where(high > 0, last_row, 0), ring_b, 1 - high)

    for base, raw, out, keep in (
        (base_own, tok, second, True), (base_a, tile_a, second_a, False), (base_b, tile_b, second_b, False),
    ):
        def step(row, carry, base=base, raw=raw, out=out, keep=keep):
            total = None
            for down in range(3):
                for along in range(3):
                    part = window[base + row + down - 1, pl.ds(left + along, cols), :]
                    part = part * weight[3 * down + along : 3 * down + along + 1, :]
                    total = part if total is None else total + part
            mixed = (raw[row].astype(jnp.float32) + total).astype(jnp.bfloat16)
            wide = mixed.astype(jnp.float32)
            at = pl.ds(pl.multiple_of(row * cols, cols), cols)
            out[at, :] = (wide * unit(wide) * gain_two).astype(jnp.bfloat16)
            if keep:
                hidden[at, :] = mixed
            return carry

        lax.fori_loop(0, rows, step, 0)


def head_units(wide, spread):
    square = wide * wide
    high = square.astype(jnp.bfloat16)
    low = (square - high.astype(jnp.float32)).astype(jnp.bfloat16)
    mean = jnp.dot(high, spread, preferred_element_type=jnp.float32)
    mean += jnp.dot(low, spread, preferred_element_type=jnp.float32)
    return (wide * lax.rsqrt(mean + EPS)).astype(jnp.bfloat16)


def spread_matrix(size, head):
    row = lax.broadcasted_iota(jnp.int32, (size, size), 0) // head
    col = lax.broadcasted_iota(jnp.int32, (size, size), 1) // head
    return jnp.where(row == col, 1.0 / head, 0.0).astype(jnp.bfloat16)


CHUNK = 256


def keys_values(tokens, w_key, w_value, keys, values, head):
    spread = spread_matrix(CHUNK, head)
    for start in range(0, w_key.shape[1], CHUNK):
        part = slice(start, start + CHUNK)
        raw = jnp.dot(tokens, w_key[:, part], preferred_element_type=jnp.float32)
        keys[:, part] = head_units(raw, spread)
        raw = jnp.dot(tokens, w_value[:, part], preferred_element_type=jnp.float32)
        values[:, part] = raw.astype(jnp.bfloat16)


def attend(queries, keys, values, pair, width, head, slots, flags, scales):
    size = queries.shape[0]
    lanes = slice(pair * width, (pair + 1) * width)
    query = queries[:, lanes]
    lane = lax.broadcasted_iota(jnp.int32, query.shape, 1)
    zero = jnp.zeros_like(query)
    both = jnp.concatenate(
        [jnp.where(lane < head, query, zero), jnp.where(lane < head, zero, query)], axis=0
    )
    scores = lax.dot_general(
        both, keys[:, lanes], (((1,), (1,)), ((), ())), preferred_element_type=jnp.float32
    )
    top, low, mixed = [], [], []
    weights = []
    for half in range(2):
        part = scores[half * size : (half + 1) * size]
        scale = scales[2 * pair + half]
        best = None
        for slot in range(slots):
            at = part[:, slot * size : (slot + 1) * size]
            peak = jnp.max(at, axis=-1, keepdims=True) - flags[slot]
            best = peak if best is None else jnp.maximum(best, peak)
        rows = []
        for slot in range(slots):
            at = part[:, slot * size : (slot + 1) * size]
            rows.append(jnp.exp2((at - (best + flags[slot])) * scale))
        exps = jnp.concatenate(rows, axis=1)
        low.append(jnp.sum(exps, axis=-1, keepdims=True))
        top.append(best * scale)
        weights.append(exps.astype(jnp.bfloat16))
    mixed = jnp.dot(
        jnp.concatenate(weights, axis=0), values[:, lanes], preferred_element_type=jnp.float32
    )
    lane = lax.broadcasted_iota(jnp.int32, (size, width), 1)
    return top, low, jnp.where(lane < head, mixed[:size], mixed[size:])


def columns(parts, size):
    lane = lax.broadcasted_iota(jnp.int32, (size, 128), 1)
    out = jnp.zeros((size, 128), jnp.float32)
    for index, part in enumerate(parts):
        out = jnp.where(lane == index, part, out)
    return out


def near_kernel(
    heads, meta, scale_in, own, own_a, own_b, on, on_a, on_b, w_query, w_key, w_value,
    query_out, top_out, low_out, mixed_out, keys, values,
):
    size, model = own.shape
    head = model // heads
    spread = spread_matrix(CHUNK, head)
    first = own[...]
    for start in range(0, model, CHUNK):
        part = slice(start, start + CHUNK)
        raw = jnp.dot(first, w_query[:, part], preferred_element_type=jnp.float32)
        query_out[:, part] = head_units(raw, spread)
    tokens = jnp.concatenate([ref[...] for ref in (own, own_a, own_b, on, on_a, on_b)], axis=0)
    keys_values(tokens, w_key, w_value, keys, values, head)
    flags = [jnp.where(meta[slot] > 0, 0.0, BIG).astype(jnp.float32) for slot in range(6)]
    factor = math.log2(math.e) / math.sqrt(head)
    scales = [scale_in[index] * factor for index in range(heads)]
    tops, lows = [], []
    for pair in range(heads // 2):
        top, low, mixed = attend(
            query_out, keys, values, pair, 2 * head, head, 6, flags, scales
        )
        tops += top
        lows += low
        mixed_out[:, 2 * head * pair : 2 * head * (pair + 1)] = mixed
    top_out[...] = columns(tops, size)
    low_out[...] = columns(lows, size)


def far_kernel(
    heads, meta, scale_in, off, off_a, off_b, off_x, on_y, w_key, w_value, w_out,
    queries, tops, lows, mixeds, hidden, result, keys, values, joined,
):
    size, model = off.shape
    head = model // heads
    polar = meta[12] > 0
    third = jnp.where(polar, off_x[...], off_b[...])
    tokens = jnp.concatenate([off[...], off_a[...], third, on_y[...]], axis=0)
    keys_values(tokens, w_key, w_value, keys, values, head)
    flags = [jnp.where(meta[6 + slot] > 0, 0.0, BIG).astype(jnp.float32) for slot in range(4)]
    factor = math.log2(math.e) / math.sqrt(head)
    scales = [scale_in[index] * factor for index in range(heads)]
    old_top, old_low = tops[...], lows[...]
    lane = lax.broadcasted_iota(jnp.int32, (size, 2 * head), 1)
    for pair in range(heads // 2):
        top, low, mixed = attend(queries, keys, values, pair, 2 * head, head, 4, flags, scales)
        before, after = [], []
        for half in range(2):
            index = 2 * pair + half
            was = old_top[:, index : index + 1]
            best = jnp.maximum(was, top[half])
            old, new = jnp.exp2(was - best), jnp.exp2(top[half] - best)
            share = 1.0 / (old * old_low[:, index : index + 1] + new * low[half])
            before.append(old * share)
            after.append(new * share)
        at = slice(2 * head * pair, 2 * head * (pair + 1))
        kept = mixeds[:, at] * jnp.where(lane < head, before[0], before[1])
        added = mixed * jnp.where(lane < head, after[0], after[1])
        joined[:, at] = (kept + added).astype(jnp.bfloat16)
    attended = joined[...]
    for start in range(0, model, CHUNK):
        part = slice(start, start + CHUNK)
        out = jnp.dot(attended, w_out[:, part], preferred_element_type=jnp.float32)
        result[:, part] = (hidden[:, part].astype(jnp.float32) + out).astype(jnp.bfloat16)


def on_device(
    tokens, norm1_gain, conv_weight, norm2_gain, w_query, w_key, w_value, w_out, head_scale, pattern
):
    rows, cols, model = tokens.shape
    size = rows * cols
    heads = head_scale.shape[0]
    lats, lons = lax.axis_size("lat"), lax.axis_size("lon")
    band, sector = lax.axis_index("lat"), lax.axis_index("lon")
    every = range(lats)
    inner = range(1, lats - 1)
    poles = (0, lats - 1)
    both = ("lat", "lon")

    swap_a = functools.partial(permuted, axis="lat", pairs=pair_swaps(lats, 0))
    swap_b = functools.partial(permuted, axis="lat", pairs=pair_swaps(lats, 1))

    def across(value, off_chip, bands=every):
        return permuted(value, both, lon_pairs(bands, lats, lons, off_chip))

    even_band = band % 2 == 0
    band_a = jnp.where(even_band, band + 1, band - 1)
    band_b = jnp.where(even_band, band - 1, band + 1)
    polar = (band == 0) | (band == lats - 1)
    even_sector = sector % 2 == 0

    def on_of(place):
        return jnp.where(place % 2 == 0, place + 1, place - 1)

    def off_of(place):
        return jnp.where(place % 2 == 0, place - 1 + lons, place + 1) % lons

    on_sector, off_sector = on_of(sector), off_of(sector)
    places = [
        (band, sector), (band_a, sector), (band_b, sector),
        (band, on_sector), (band_a, on_sector), (band_b, on_sector),
        (band, off_sector), (band_a, off_sector),
        (jnp.where(polar, band, band_b), jnp.where(polar, on_of(off_sector), off_sector)),
        (band, off_of(on_sector)),
    ]
    ids = jnp.stack([at_band * lons + at_sector for at_band, at_sector in places])
    exists = [True, True, ~polar, True, True, ~polar, True, True, True, polar]
    exists = jnp.stack([jnp.asarray(flag) for flag in exists])
    listed = jnp.any(pattern.reshape(-1)[None, :] == ids[:, None], axis=1) & exists
    extra = jnp.stack([~even_band, band % 4 >= 2, polar])
    meta = jnp.concatenate([listed, extra]).astype(jnp.int32)

    tile_a, tile_b = swap_a(tokens), swap_b(tokens)
    edges = jnp.concatenate([tokens[:, 0], tokens[:, cols - 1]], axis=0)
    on_edges, off_edges = across(edges, False), across(edges, True)
    halo = jnp.concatenate(
        [
            jnp.where(even_sector, off_edges[rows:], on_edges[rows:]),
            jnp.where(even_sector, on_edges[:rows], off_edges[:rows]),
        ],
        axis=0,
    )
    halo_a, halo_b = swap_a(halo), swap_b(halo)
    brink = jnp.concatenate([tokens[0], tokens[rows - 1], halo], axis=0)
    ring_a = permuted(brink, "lat", two_away(lats, 0))
    ring_b = permuted(brink, "lat", two_away(lats, 2))

    tile = jax.ShapeDtypeStruct((size, model), jnp.bfloat16)
    limit = pltpu.CompilerParams(vmem_limit_bytes=40 * 2**20)
    hidden, second, second_a, second_b = pl.pallas_call(
        conv_kernel,
        out_shape=[tile] * 4,
        in_specs=[SMEM] + [VMEM] * 11,
        out_specs=[VMEM] * 4,
        scratch_shapes=[pltpu.VMEM((2 + 3 * rows, 32, model), jnp.float32)],
        compiler_params=limit,
        name="conv",
    )(
        meta, tokens, tile_a, tile_b, halo, halo_a, halo_b, ring_a, ring_b,
        norm1_gain.reshape(1, model), conv_weight.reshape(9, model), norm2_gain.reshape(1, model),
    )

    on, on_a, on_b = across(second, False), across(second_a, False), across(second_b, False)
    off = across(second, True)
    off_a = across(second_a, True)
    off_b = across(second_b, True, inner)
    off_x = across(on, True, poles)
    on_y = across(off, False, poles)

    stats = jax.ShapeDtypeStruct((size, 128), jnp.float32)
    queries, tops, lows, mixed = pl.pallas_call(
        functools.partial(near_kernel, heads),
        out_shape=[tile, stats, stats, jax.ShapeDtypeStruct((size, model), jnp.float32)],
        in_specs=[SMEM, SMEM] + [VMEM] * 9,
        out_specs=[VMEM] * 4,
        scratch_shapes=[pltpu.VMEM((6 * size, model), jnp.bfloat16)] * 2,
        compiler_params=limit,
        cost_estimate=pl.CostEstimate(
            flops=2 * size * model * model * 13, bytes_accessed=8 * 2**20, transcendentals=0
        ),
        name="near",
    )(meta, head_scale, second, second_a, second_b, on, on_a, on_b, w_query, w_key, w_value)

    result = pl.pallas_call(
        functools.partial(far_kernel, heads),
        out_shape=tile,
        in_specs=[SMEM, SMEM] + [VMEM] * 13,
        out_specs=VMEM,
        scratch_shapes=[pltpu.VMEM((4 * size, model), jnp.bfloat16)] * 2
        + [pltpu.VMEM((size, model), jnp.bfloat16)],
        compiler_params=limit,
        cost_estimate=pl.CostEstimate(
            flops=2 * size * model * model * 9, bytes_accessed=8 * 2**20, transcendentals=0
        ),
        name="far",
    )(
        meta, head_scale, off, off_a, off_b, off_x, on_y, w_key, w_value, w_out,
        queries, tops, lows, mixed, hidden,
    )
    return result.reshape(rows, cols, model)


def solution(mesh):
    return jax.shard_map(
        on_device,
        mesh=mesh,
        in_specs=(
            P("lat", "lon", None),
            P(),
            P(),
            P(),
            P(),
            P(),
            P(),
            P(),
            P(),
            P("lat", "lon", None),
        ),
        out_specs=P("lat", "lon", None),
        check_vma=False,
    )
```

```python
import functools
import math

import jax
import jax.numpy as jnp
from jax import lax
from jax.experimental import pallas as pl
from jax.experimental.pallas import tpu as pltpu
from jax.sharding import PartitionSpec as P

EPS = 1e-06
BIG = 1e30
VMEM = pl.BlockSpec(memory_space=pltpu.VMEM)
SMEM = pl.BlockSpec(memory_space=pltpu.SMEM)


def pair_swaps(count, first):
    pairs = []
    for low in range(first, count - 1, 2):
        pairs += [(low, low + 1), (low + 1, low)]
    return pairs


def lon_pairs(lats, lat_count, lon_count, off_chip):
    pairs = []
    for lat in lats:
        for low in range(1 if off_chip else 0, lon_count, 2):
            one, two = lat * lon_count + low, lat * lon_count + (low + 1) % lon_count
            pairs += [(one, two), (two, one)]
    return pairs


def two_away(count, first):
    pairs = []
    for start in range(first, count, 4):
        for low in (start, start + 1):
            if low + 2 < count:
                pairs += [(low, low + 2), (low + 2, low)]
    return pairs


def permuted(value, axis, pairs):
    if not pairs:
        return jnp.zeros_like(value)
    return lax.ppermute(value, axis, pairs)


def unit(values):
    return lax.rsqrt(jnp.mean(values * values, axis=-1, keepdims=True) + EPS)


def partner(place, count, off_chip):
    even = place % 2 == 0
    if not off_chip:
        return jnp.where(even, place + 1, place - 1)
    return jnp.where(even, jnp.where(place == 0, count - 1, place - 1), jnp.where(place == count - 1, 0, place + 1))


def band_facts():
    lats = lax.axis_size("lat")
    band = lax.axis_index("lat")
    even = band % 2 == 0
    polar = (band == 0) | (band == lats - 1)
    return band, jnp.where(even, band + 1, band - 1), jnp.where(even, band - 1, band + 1), polar


def slot_penalties(pattern, slots):
    lons = lax.axis_size("lon")
    band, band_a, band_b, polar = band_facts()
    sector = lax.axis_index("lon")
    on, off = partner(sector, lons, False), partner(sector, lons, True)
    places = [
        (band, sector), (band_a, sector), (band_b, sector),
        (band, on), (band_a, on), (band_b, on),
        (band, off), (band_a, off),
        (jnp.where(polar, band, band_b), jnp.where(polar, partner(off, lons, False), off)),
        (jnp.where(polar, band, band_b), jnp.where(polar, partner(on, lons, True), sector)),
    ]
    exists = {2: ~polar, 5: ~polar}
    out = []
    for slot in slots:
        tile = places[slot][0] * lons + places[slot][1]
        listed = pattern[0] == tile
        for index in range(1, pattern.shape[0]):
            listed = listed | (pattern[index] == tile)
        if slot in exists:
            listed = listed & exists[slot]
        out.append(jnp.where(listed, 0.0, BIG).astype(jnp.float32))
    return out


def prep_kernel(tok, tok_out, edges, brink):
    rows, cols, width = tok.shape
    tok_out[...] = tok[...]
    first = lax.broadcasted_iota(jnp.int32, (2 * rows, width), 0)
    out = jnp.zeros((2 * rows, width), jnp.float32)
    for row in range(rows):
        line = tok[row].astype(jnp.float32)
        out = jnp.where(first == row, line[0:1], out)
        out = jnp.where(first == rows + row, line[cols - 1 : cols], out)
    edges[...] = out.astype(edges.dtype)
    brink[:cols, :] = tok[0]
    brink[cols:, :] = tok[rows - 1]


def conv_kernel(
    tok, tile_a, tile_b, halo, halo_a, halo_b, ring_a, ring_b, gains,
    hidden, second, second_a, second_b, before, middle, after, mixed,
):
    rows, cols, width = tok.shape
    gain_one, gain_two = gains[0:1, :], gains[1:2, :]
    place = lax.broadcasted_iota(jnp.int32, (cols, width), 0)

    def normed(raw):
        wide = raw.astype(jnp.float32)
        return (wide * unit(wide) * gain_one).astype(jnp.bfloat16).astype(jnp.float32)

    def put(row, value, left, right):
        middle[row] = value
        before[row] = jnp.where(place == 0, left, pltpu.roll(value, 1, 0))
        after[row] = jnp.where(place == cols - 1, right, pltpu.roll(value, cols - 1, 0))

    def tile_rows(base, raw, edges):
        sides = normed(edges[...])
        for row in range(rows):
            put(base + row, normed(raw[row]), sides[row : row + 1], sides[rows + row : rows + row + 1])

    def ring(row, data, bottom):
        base = pl.multiple_of(bottom * cols, cols)
        sides = normed(data[2 * cols :, :])
        left = jnp.where(bottom > 0, sides[rows - 1 : rows], sides[0:1])
        right = jnp.where(bottom > 0, sides[2 * rows - 1 : 2 * rows], sides[rows : rows + 1])
        put(row, normed(data[pl.ds(base, cols), :]), left, right)

    band = lax.axis_index("lat")
    odd = band % 2
    high = (band // 2) % 2
    base_own = 1 + rows
    base_a = jnp.where(odd > 0, 1, 1 + 2 * rows)
    base_b = jnp.where(odd > 0, 1 + 2 * rows, 1)
    last_row = 1 + 3 * rows
    tile_rows(base_own, tok, halo)
    tile_rows(base_a, tile_a, halo_a)
    tile_rows(base_b, tile_b, halo_b)
    ring(jnp.where(high > 0, 0, last_row), ring_a, high)
    ring(jnp.where(high > 0, last_row, 0), ring_b, 1 - high)

    for base, raw, out, keep in (
        (base_own, tok, second, True), (base_a, tile_a, second_a, False), (base_b, tile_b, second_b, False),
    ):
        for start in range(0, width, 256):
            lanes = slice(start, start + 256)
            taps = [gains[2 + index : 3 + index, lanes] for index in range(9)]
            totals = [None] * rows
            for row in range(-1, rows + 1):
                parts = [ref[base + row, :, lanes] for ref in (before, middle, after)]
                for target in range(max(row - 1, 0), min(row + 2, rows)):
                    for along in range(3):
                        term = parts[along] * taps[3 * (row - target + 1) + along]
                        totals[target] = term if totals[target] is None else totals[target] + term
            for row in range(rows):
                mixed[row * cols : (row + 1) * cols, lanes] = (
                    raw[row, :, lanes].astype(jnp.float32) + totals[row]
                ).astype(jnp.bfloat16)
        if keep:
            hidden[...] = mixed[...]
        for row in range(rows):
            at = slice(row * cols, (row + 1) * cols)
            wide = mixed[at, :].astype(jnp.float32)
            out[at, :] = (wide * unit(wide) * gain_two).astype(jnp.bfloat16)


def head_marks(model, head):
    channel = lax.broadcasted_iota(jnp.int32, (model, 128), 0) // head
    index = lax.broadcasted_iota(jnp.int32, (model, 128), 1) % 64
    return jnp.where(channel == index, 1.0, 0.0).astype(jnp.bfloat16)


def head_units(wide, marks, head):
    square = (wide * wide).astype(jnp.bfloat16)
    total = jnp.dot(square, marks, preferred_element_type=jnp.float32)
    share = lax.rsqrt(total * (1.0 / head) + EPS)
    high = share.astype(jnp.bfloat16).astype(jnp.float32)
    lane = lax.broadcasted_iota(jnp.int32, share.shape, 1)
    split = jnp.where(lane < 64, high, share - high).astype(jnp.bfloat16)
    factor = lax.dot_general(
        split, marks, (((1,), (1,)), ((), ())), preferred_element_type=jnp.float32
    )
    return (wide * factor).astype(jnp.bfloat16)


CHUNK = 256


def group_kernel(heads, slots, first, last, *refs):
    refs = list(refs)

    def take(count):
        out = refs[:count]
        del refs[:count]
        return out

    pattern, scale_in = take(2)
    tiles = take(len(slots) + last)
    w_key, w_value = take(2)
    if first:
        (w_query,) = take(1)
    else:
        queries, tops, lows, sums = take(4)
    if last:
        w_out, hidden, result = take(3)
    else:
        if first:
            (queries,) = take(1)
        tops_out, lows_out, sums_out = take(3)
    keys, values = take(2)
    if last:
        (joined,) = take(1)

    size, model = tiles[0].shape
    head = model // heads
    width = 2 * head
    marks = head_marks(model, head)
    if first:
        raw = jnp.dot(tiles[0][...], w_query[...], preferred_element_type=jnp.float32)
        queries[...] = head_units(raw, marks, head)
    tokens = [ref[...] for ref in tiles]
    if last:
        other = tokens.pop()
        tokens[-1] = jnp.where(band_facts()[3], tokens[-1], other)
    tokens = jnp.concatenate(tokens, axis=0)
    raw = jnp.dot(tokens, w_key[...], preferred_element_type=jnp.float32)
    keys[...] = head_units(raw, marks, head)
    values[...] = lax.dot_general(
        w_value[...], tokens, (((1,), (1,)), ((), ())), preferred_element_type=jnp.float32
    ).astype(jnp.bfloat16)

    flags = slot_penalties(pattern, slots)
    factor = math.log2(math.e) / math.sqrt(head)
    lane = lax.broadcasted_iota(jnp.int32, (size, width), 1)
    half = lax.broadcasted_iota(jnp.int32, (1, 2 * size), 1) < size
    for pair in range(heads // 2):
        lanes = slice(pair * width, (pair + 1) * width)
        query = queries[:, lanes]
        zero = jnp.zeros_like(query)
        both = jnp.concatenate(
            [jnp.where(lane < head, query, zero), jnp.where(lane < head, zero, query)], axis=0
        )
        scores = lax.dot_general(
            keys[:, lanes], both, (((1,), (1,)), ((), ())), preferred_element_type=jnp.float32
        )
        scale = jnp.where(half, scale_in[2 * pair] * factor, scale_in[2 * pair + 1] * factor)
        parts = [scores[slot * size : (slot + 1) * size] * scale for slot in range(len(slots))]
        best = None if first else tops[pair : pair + 1, :]
        for part, flag in zip(parts, flags):
            peak = jnp.max(part, axis=0, keepdims=True) - flag
            best = peak if best is None else jnp.maximum(best, peak)
        exps = [jnp.exp2(part - (best + flag)) for part, flag in zip(parts, flags)]
        total = exps[0]
        for part in exps[1:]:
            total = total + part
        low = jnp.sum(total, axis=0, keepdims=True)
        weights = jnp.concatenate([part.astype(jnp.bfloat16) for part in exps], axis=0)
        mixed = jnp.dot(values[lanes, :], weights, preferred_element_type=jnp.float32)
        mixed = jnp.concatenate([mixed[:head, :size], mixed[head:, size:]], axis=0)
        if not first:
            old = jnp.exp2(tops[pair : pair + 1, :] - best)
            low = low + old * lows[pair : pair + 1, :]
            mixed = mixed + sums[lanes, :] * spans(old, size, head)
        if last:
            joined[:, lanes] = jnp.transpose(mixed * spans(1.0 / low, size, head)).astype(jnp.bfloat16)
        else:
            sums_out[lanes, :] = mixed
            tops_out[pair : pair + 1, :] = best
            lows_out[pair : pair + 1, :] = low
    if not last:
        return
    attended = joined[...]
    for start in range(0, model, CHUNK):
        part = slice(start, start + CHUNK)
        out = jnp.dot(attended, w_out[:, part], preferred_element_type=jnp.float32)
        result[:, part] = (hidden[:, part].astype(jnp.float32) + out).astype(jnp.bfloat16)


def spans(row, size, head):
    return jnp.concatenate(
        [jnp.broadcast_to(row[:, :size], (head, size)), jnp.broadcast_to(row[:, size:], (head, size))],
        axis=0,
    )


def limit(mebibytes):
    return pltpu.CompilerParams(vmem_limit_bytes=mebibytes * 2**20)


def attend(heads, slots, pattern, scale, tiles, weights, state, finish):
    first, last = state is None, finish is not None
    size, model = tiles[0].shape
    tile = jax.ShapeDtypeStruct((size, model), jnp.bfloat16)
    stats = jax.ShapeDtypeStruct((heads // 2, 2 * size), jnp.float32)
    out = [stats, stats, jax.ShapeDtypeStruct((model, size), jnp.float32)]
    if last:
        out = [tile]
    elif first:
        out = [tile] + out
    operands = [pattern, scale, *tiles, *weights]
    if not first:
        operands += list(state)
    if last:
        operands += list(finish)
    scratch = [
        pltpu.VMEM((len(slots) * size, model), jnp.bfloat16),
        pltpu.VMEM((model, len(slots) * size), jnp.bfloat16),
    ]
    if last:
        scratch.append(pltpu.VMEM((size, model), jnp.bfloat16))
    return pl.pallas_call(
        functools.partial(group_kernel, heads, slots, first, last),
        out_shape=out,
        in_specs=[SMEM, SMEM] + [VMEM] * (len(operands) - 2),
        out_specs=[VMEM] * len(out),
        scratch_shapes=scratch,
        compiler_params=limit(16),
        cost_estimate=pl.CostEstimate(
            flops=2**36, bytes_accessed=2**28, transcendentals=0
        ),
        name="attend" + "_".join(str(slot) for slot in slots),
    )(*operands)


def on_device(
    tokens, norm1_gain, conv_weight, norm2_gain, w_query, w_key, w_value, w_out, head_scale, pattern
):
    rows, cols, model = tokens.shape
    size = rows * cols
    heads = head_scale.shape[0]
    lats, lons = lax.axis_size("lat"), lax.axis_size("lon")
    polar = band_facts()[3]
    even_sector = lax.axis_index("lon") % 2 == 0
    lists = pattern.reshape(-1)

    swap_a = functools.partial(permuted, axis="lat", pairs=pair_swaps(lats, 0))
    swap_b = functools.partial(permuted, axis="lat", pairs=pair_swaps(lats, 1))

    def across(value, off_chip):
        return permuted(value, ("lat", "lon"), lon_pairs(range(lats), lats, lons, off_chip))

    tile_a, tile_b = swap_a(tokens), swap_b(tokens)
    tok, edges, brink = pl.pallas_call(
        prep_kernel,
        out_shape=[
            jax.ShapeDtypeStruct(shape, tokens.dtype)
            for shape in (tokens.shape, (2 * rows, model), (2 * cols, model))
        ],
        in_specs=[VMEM],
        out_specs=[VMEM] * 3,
        compiler_params=limit(2),
        cost_estimate=pl.CostEstimate(flops=0, bytes_accessed=2**21, transcendentals=0),
        name="prep",
    )(tokens)
    gains = jnp.concatenate(
        [norm1_gain.reshape(1, model), norm2_gain.reshape(1, model), conv_weight.reshape(9, model)],
        axis=0,
    )
    on_edges, off_edges = across(edges, False), across(edges, True)
    halo = jnp.concatenate(
        [
            jnp.where(even_sector, off_edges[rows:], on_edges[rows:]),
            jnp.where(even_sector, on_edges[:rows], off_edges[:rows]),
        ],
        axis=0,
    )
    halo_a, halo_b = swap_a(halo), swap_b(halo)
    brink = jnp.concatenate([brink, halo], axis=0)
    ring_a = permuted(brink, "lat", two_away(lats, 0))
    ring_b = permuted(brink, "lat", two_away(lats, 2))

    tile = jax.ShapeDtypeStruct((size, model), jnp.bfloat16)
    w_value = jnp.transpose(w_value)
    gains, w_value = lax.optimization_barrier((gains, w_value))
    window = pltpu.VMEM((2 + 3 * rows, cols, model), jnp.float32)
    hidden, second, second_a, second_b = pl.pallas_call(
        conv_kernel,
        out_shape=[tile] * 4,
        in_specs=[VMEM] * 9,
        out_specs=[VMEM] * 4,
        scratch_shapes=[window] * 3 + [pltpu.VMEM((size, model), jnp.bfloat16)],
        compiler_params=limit(10),
        cost_estimate=pl.CostEstimate(flops=2**24, bytes_accessed=24 * 2**20, transcendentals=0),
        name="conv",
    )(
        tok, tile_a, tile_b, halo, halo_a, halo_b, ring_a, ring_b, gains
    )

    on = across(second, False)
    off = across(second, True)
    on_a, on_b = across(second_a, False), across(second_b, False)
    off_a = across(second_a, True)
    third = across(jnp.where(polar, on, second_b), True)

    queries, *state = attend(
        heads, (0, 1, 3, 4, 5), lists, head_scale, [second, second_a, on, on_a, on_b],
        [w_key, w_value, w_query], None, None,
    )
    off, queries = lax.optimization_barrier((off, queries))
    on_y = across(off, False)
    (result,) = attend(
        heads, (6, 7, 8, 9), lists, head_scale, [off, off_a, third, on_y, second_b], [w_key, w_value],
        [queries, *state], [w_out, hidden],
    )
    return result.reshape(rows, cols, model)


def solution(mesh):
    return jax.shard_map(
        on_device,
        mesh=mesh,
        in_specs=(
            P("lat", "lon", None),
            P(),
            P(),
            P(),
            P(),
            P(),
            P(),
            P(),
            P(),
            P("lat", "lon", None),
        ),
        out_specs=P("lat", "lon", None),
        check_vma=False,
    )
```

```python
import functools
import math

import jax
import jax.numpy as jnp
from jax import lax
from jax.experimental import pallas as pl
from jax.experimental.pallas import tpu as pltpu
from jax.sharding import PartitionSpec as P

EPS = 1e-06
BIG = 1e30
VMEM = pl.BlockSpec(memory_space=pltpu.VMEM)
SMEM = pl.BlockSpec(memory_space=pltpu.SMEM)


def pair_swaps(count, first):
    pairs = []
    for low in range(first, count - 1, 2):
        pairs += [(low, low + 1), (low + 1, low)]
    return pairs


def lon_pairs(lats, lat_count, lon_count, off_chip):
    pairs = []
    for lat in lats:
        for low in range(1 if off_chip else 0, lon_count, 2):
            one, two = lat * lon_count + low, lat * lon_count + (low + 1) % lon_count
            pairs += [(one, two), (two, one)]
    return pairs


def two_away(count, first):
    pairs = []
    for start in range(first, count, 4):
        for low in (start, start + 1):
            if low + 2 < count:
                pairs += [(low, low + 2), (low + 2, low)]
    return pairs


def permuted(value, axis, pairs):
    if not pairs:
        return jnp.zeros_like(value)
    return lax.ppermute(value, axis, pairs)


def unit(values):
    return lax.rsqrt(jnp.mean(values * values, axis=-1, keepdims=True) + EPS)


def partner(place, count, off_chip):
    even = place % 2 == 0
    if not off_chip:
        return jnp.where(even, place + 1, place - 1)
    return jnp.where(even, jnp.where(place == 0, count - 1, place - 1), jnp.where(place == count - 1, 0, place + 1))


def band_facts():
    lats = lax.axis_size("lat")
    band = lax.axis_index("lat")
    even = band % 2 == 0
    polar = (band == 0) | (band == lats - 1)
    return band, jnp.where(even, band + 1, band - 1), jnp.where(even, band - 1, band + 1), polar


def slot_penalties(pattern, slots):
    lons = lax.axis_size("lon")
    band, band_a, band_b, polar = band_facts()
    sector = lax.axis_index("lon")
    on, off = partner(sector, lons, False), partner(sector, lons, True)
    places = [
        (band, sector), (band_a, sector), (band_b, sector),
        (band, on), (band_a, on), (band_b, on),
        (band, off), (band_a, off),
        (jnp.where(polar, band, band_b), jnp.where(polar, partner(off, lons, False), off)),
        (jnp.where(polar, band, band_b), jnp.where(polar, partner(on, lons, True), sector)),
    ]
    exists = {2: ~polar, 5: ~polar}
    out = []
    for slot in slots:
        tile = places[slot][0] * lons + places[slot][1]
        listed = pattern[0] == tile
        for index in range(1, pattern.shape[0]):
            listed = listed | (pattern[index] == tile)
        if slot in exists:
            listed = listed & exists[slot]
        out.append(jnp.where(listed, 0.0, BIG).astype(jnp.float32))
    return out


def prep_kernel(tok, tok_out, edges, brink):
    rows, cols, width = tok.shape
    tok_out[...] = tok[...]
    first = lax.broadcasted_iota(jnp.int32, (2 * rows, width), 0)
    out = jnp.zeros((2 * rows, width), jnp.float32)
    for row in range(rows):
        line = tok[row].astype(jnp.float32)
        out = jnp.where(first == row, line[0:1], out)
        out = jnp.where(first == rows + row, line[cols - 1 : cols], out)
    edges[...] = out.astype(edges.dtype)
    brink[:cols, :] = tok[0]
    brink[cols:, :] = tok[rows - 1]


def conv_kernel(
    tok, tile_a, tile_b, halo, halo_a, halo_b, ring_a, ring_b, gains,
    hidden, second, second_a, second_b, copy_b, before, middle, after, mixed,
):
    rows, cols, width = tok.shape
    gain_one, gain_two = gains[0:1, :], gains[1:2, :]
    place = lax.broadcasted_iota(jnp.int32, (cols, width), 0)

    def normed(raw):
        wide = raw.astype(jnp.float32)
        return (wide * unit(wide) * gain_one).astype(jnp.bfloat16).astype(jnp.float32)

    def put(row, value, left, right):
        middle[row] = value
        before[row] = jnp.where(place == 0, left, pltpu.roll(value, 1, 0))
        after[row] = jnp.where(place == cols - 1, right, pltpu.roll(value, cols - 1, 0))

    def tile_rows(base, raw, edges):
        sides = normed(edges[...])
        for row in range(rows):
            put(base + row, normed(raw[row]), sides[row : row + 1], sides[rows + row : rows + row + 1])

    def ring(row, data, bottom):
        base = pl.multiple_of(bottom * cols, cols)
        sides = normed(data[2 * cols :, :])
        left = jnp.where(bottom > 0, sides[rows - 1 : rows], sides[0:1])
        right = jnp.where(bottom > 0, sides[2 * rows - 1 : 2 * rows], sides[rows : rows + 1])
        put(row, normed(data[pl.ds(base, cols), :]), left, right)

    band = lax.axis_index("lat")
    odd = band % 2
    high = (band // 2) % 2
    base_own = 1 + rows
    base_a = jnp.where(odd > 0, 1, 1 + 2 * rows)
    base_b = jnp.where(odd > 0, 1 + 2 * rows, 1)
    last_row = 1 + 3 * rows
    tile_rows(base_own, tok, halo)
    tile_rows(base_a, tile_a, halo_a)
    tile_rows(base_b, tile_b, halo_b)
    ring(jnp.where(high > 0, 0, last_row), ring_a, high)
    ring(jnp.where(high > 0, last_row, 0), ring_b, 1 - high)

    for base, raw, out, keep in (
        (base_own, tok, second, True), (base_a, tile_a, second_a, False), (base_b, tile_b, second_b, False),
    ):
        for start in range(0, width, 256):
            lanes = slice(start, start + 256)
            taps = [gains[2 + index : 3 + index, lanes] for index in range(9)]
            totals = [None] * rows
            for row in range(-1, rows + 1):
                parts = [ref[base + row, :, lanes] for ref in (before, middle, after)]
                for target in range(max(row - 1, 0), min(row + 2, rows)):
                    for along in range(3):
                        term = parts[along] * taps[3 * (row - target + 1) + along]
                        totals[target] = term if totals[target] is None else totals[target] + term
            for row in range(rows):
                mixed[row * cols : (row + 1) * cols, lanes] = (
                    raw[row, :, lanes].astype(jnp.float32) + totals[row]
                ).astype(jnp.bfloat16)
        if keep:
            hidden[...] = mixed[...]
        for row in range(rows):
            at = slice(row * cols, (row + 1) * cols)
            wide = mixed[at, :].astype(jnp.float32)
            out[at, :] = (wide * unit(wide) * gain_two).astype(jnp.bfloat16)
    copy_b[...] = second_b[...]


def head_marks(model, head):
    channel = lax.broadcasted_iota(jnp.int32, (model, 128), 0) // head
    index = lax.broadcasted_iota(jnp.int32, (model, 128), 1) % 64
    return jnp.where(channel == index, 1.0, 0.0).astype(jnp.bfloat16)


def head_units(wide, marks, head):
    square = (wide * wide).astype(jnp.bfloat16)
    total = jnp.dot(square, marks, preferred_element_type=jnp.float32)
    share = lax.rsqrt(total * (1.0 / head) + EPS)
    high = share.astype(jnp.bfloat16).astype(jnp.float32)
    lane = lax.broadcasted_iota(jnp.int32, share.shape, 1)
    split = jnp.where(lane < 64, high, share - high).astype(jnp.bfloat16)
    factor = lax.dot_general(
        split, marks, (((1,), (1,)), ((), ())), preferred_element_type=jnp.float32
    )
    return (wide * factor).astype(jnp.bfloat16)


CHUNK = 256


def group_kernel(heads, slots, first, last, *refs):
    refs = list(refs)

    def take(count):
        out = refs[:count]
        del refs[:count]
        return out

    pattern, scale_in = take(2)
    tiles = take(len(slots) + last)
    w_key, w_value = take(2)
    if first:
        (w_query,) = take(1)
    else:
        queries, tops, lows, sums = take(4)
    if last:
        w_out, hidden, result = take(3)
    else:
        if first:
            (queries,) = take(1)
        tops_out, lows_out, sums_out = take(3)
    keys, values = take(2)
    if last:
        (joined,) = take(1)

    size, model = tiles[0].shape
    head = model // heads
    width = 2 * head
    marks = head_marks(model, head)
    if first:
        raw_query = jnp.dot(tiles[0][...], w_query[...], preferred_element_type=jnp.float32)
    tokens = [ref[...] for ref in tiles]
    if last:
        other = tokens.pop()
        tokens[-1] = jnp.where(band_facts()[3], tokens[-1], other)
    tokens = jnp.concatenate(tokens, axis=0)
    held = None
    for start in range(0, model, CHUNK):
        part = slice(start, start + CHUNK)
        raw = jnp.dot(tokens, w_key[:, part], preferred_element_type=jnp.float32)
        if held is not None:
            keys[:, held[0]] = head_units(held[1], marks[:CHUNK], head)
        elif first:
            queries[...] = head_units(raw_query, marks, head)
        held = (part, raw)
    values[...] = lax.dot_general(
        w_value[...], tokens, (((1,), (1,)), ((), ())), preferred_element_type=jnp.float32
    ).astype(jnp.bfloat16)
    keys[:, held[0]] = head_units(held[1], marks[:CHUNK], head)

    flags = slot_penalties(pattern, slots)
    factor = math.log2(math.e) / math.sqrt(head)
    lane = lax.broadcasted_iota(jnp.int32, (size, width), 1)
    half = lax.broadcasted_iota(jnp.int32, (1, 2 * size), 1) < size
    def weigh(pair):
        lanes = slice(pair * width, (pair + 1) * width)
        query = queries[:, lanes]
        zero = jnp.zeros_like(query)
        both = jnp.concatenate(
            [jnp.where(lane < head, query, zero), jnp.where(lane < head, zero, query)], axis=0
        )
        scores = lax.dot_general(
            keys[:, lanes], both, (((1,), (1,)), ((), ())), preferred_element_type=jnp.float32
        )
        scale = jnp.where(half, scale_in[2 * pair] * factor, scale_in[2 * pair + 1] * factor)
        parts = [scores[slot * size : (slot + 1) * size] * scale for slot in range(len(slots))]
        best = None if first else tops[pair : pair + 1, :]
        for part, flag in zip(parts, flags):
            peak = jnp.max(part, axis=0, keepdims=True) - flag
            best = peak if best is None else jnp.maximum(best, peak)
        exps = [jnp.exp2(part - (best + flag)) for part, flag in zip(parts, flags)]
        total = exps[0]
        for part in exps[1:]:
            total = total + part
        low = jnp.sum(total, axis=0, keepdims=True)
        return best, low, jnp.concatenate([part.astype(jnp.bfloat16) for part in exps], axis=0)

    def mix(pair, best, low, weights):
        lanes = slice(pair * width, (pair + 1) * width)
        mixed = jnp.dot(values[lanes, :], weights, preferred_element_type=jnp.float32)
        mixed = jnp.concatenate([mixed[:head, :size], mixed[head:, size:]], axis=0)
        if not first:
            old = jnp.exp2(tops[pair : pair + 1, :] - best)
            low = low + old * lows[pair : pair + 1, :]
            mixed = mixed + sums[lanes, :] * spans(old, size, head)
        if last:
            joined[:, lanes] = jnp.transpose(mixed * spans(1.0 / low, size, head)).astype(jnp.bfloat16)
        else:
            sums_out[lanes, :] = mixed
            tops_out[pair : pair + 1, :] = best
            lows_out[pair : pair + 1, :] = low

    waiting = []
    for pair in range(heads // 2):
        waiting.append((pair, *weigh(pair)))
        if len(waiting) > 2:
            mix(*waiting.pop(0))
    for entry in waiting:
        mix(*entry)
    if not last:
        return
    attended = joined[...]
    for start in range(0, model, CHUNK):
        part = slice(start, start + CHUNK)
        out = jnp.dot(attended, w_out[:, part], preferred_element_type=jnp.float32)
        result[:, part] = (hidden[:, part].astype(jnp.float32) + out).astype(jnp.bfloat16)


def spans(row, size, head):
    return jnp.concatenate(
        [jnp.broadcast_to(row[:, :size], (head, size)), jnp.broadcast_to(row[:, size:], (head, size))],
        axis=0,
    )


def limit(mebibytes):
    return pltpu.CompilerParams(vmem_limit_bytes=mebibytes * 2**20)


def attend(heads, slots, pattern, scale, tiles, weights, state, finish):
    first, last = state is None, finish is not None
    size, model = tiles[0].shape
    tile = jax.ShapeDtypeStruct((size, model), jnp.bfloat16)
    stats = jax.ShapeDtypeStruct((heads // 2, 2 * size), jnp.float32)
    out = [stats, stats, jax.ShapeDtypeStruct((model, size), jnp.float32)]
    if last:
        out = [tile]
    elif first:
        out = [tile] + out
    operands = [pattern, scale, *tiles, *weights]
    if not first:
        operands += list(state)
    if last:
        operands += list(finish)
    scratch = [
        pltpu.VMEM((len(slots) * size, model), jnp.bfloat16),
        pltpu.VMEM((model, len(slots) * size), jnp.bfloat16),
    ]
    if last:
        scratch.append(pltpu.VMEM((size, model), jnp.bfloat16))
    return pl.pallas_call(
        functools.partial(group_kernel, heads, slots, first, last),
        out_shape=out,
        in_specs=[SMEM, SMEM] + [VMEM] * (len(operands) - 2),
        out_specs=[VMEM] * len(out),
        scratch_shapes=scratch,
        compiler_params=limit(16),
        cost_estimate=pl.CostEstimate(
            flops=2**36, bytes_accessed=2**28, transcendentals=0
        ),
        name="attend" + "_".join(str(slot) for slot in slots),
    )(*operands)


def on_device(
    tokens, norm1_gain, conv_weight, norm2_gain, w_query, w_key, w_value, w_out, head_scale, pattern
):
    rows, cols, model = tokens.shape
    size = rows * cols
    heads = head_scale.shape[0]
    lats, lons = lax.axis_size("lat"), lax.axis_size("lon")
    polar = band_facts()[3]
    even_sector = lax.axis_index("lon") % 2 == 0
    lists = pattern.reshape(-1)

    swap_a = functools.partial(permuted, axis="lat", pairs=pair_swaps(lats, 0))
    swap_b = functools.partial(permuted, axis="lat", pairs=pair_swaps(lats, 1))

    def across(value, off_chip):
        return permuted(value, ("lat", "lon"), lon_pairs(range(lats), lats, lons, off_chip))

    tile_a, tile_b = swap_a(tokens), swap_b(tokens)
    tok, edges, brink = pl.pallas_call(
        prep_kernel,
        out_shape=[
            jax.ShapeDtypeStruct(shape, tokens.dtype)
            for shape in (tokens.shape, (2 * rows, model), (2 * cols, model))
        ],
        in_specs=[VMEM],
        out_specs=[VMEM] * 3,
        compiler_params=limit(2),
        cost_estimate=pl.CostEstimate(flops=0, bytes_accessed=2**21, transcendentals=0),
        name="prep",
    )(tokens)
    gains = jnp.concatenate(
        [norm1_gain.reshape(1, model), norm2_gain.reshape(1, model), conv_weight.reshape(9, model)],
        axis=0,
    )
    on_edges, off_edges = across(edges, False), across(edges, True)
    halo = jnp.concatenate(
        [
            jnp.where(even_sector, off_edges[rows:], on_edges[rows:]),
            jnp.where(even_sector, on_edges[:rows], off_edges[:rows]),
        ],
        axis=0,
    )
    halo_a, halo_b = swap_a(halo), swap_b(halo)
    brink = jnp.concatenate([brink, halo], axis=0)
    ring_a = permuted(brink, "lat", two_away(lats, 0))
    ring_b = permuted(brink, "lat", two_away(lats, 2))

    tile = jax.ShapeDtypeStruct((size, model), jnp.bfloat16)
    w_value = jnp.transpose(w_value)
    gains, w_value = lax.optimization_barrier((gains, w_value))
    window = pltpu.VMEM((2 + 3 * rows, cols, model), jnp.float32)
    hidden, second, second_a, second_b, copy_b = pl.pallas_call(
        conv_kernel,
        out_shape=[tile] * 5,
        in_specs=[VMEM] * 9,
        out_specs=[VMEM] * 5,
        scratch_shapes=[window] * 3 + [pltpu.VMEM((size, model), jnp.bfloat16)],
        compiler_params=limit(10),
        cost_estimate=pl.CostEstimate(flops=2**24, bytes_accessed=24 * 2**20, transcendentals=0),
        name="conv",
    )(
        tok, tile_a, tile_b, halo, halo_a, halo_b, ring_a, ring_b, gains
    )

    on = across(second, False)
    off = across(second, True)
    on_a, on_b = across(second_a, False), across(copy_b, False)
    off_a = across(second_a, True)
    third = across(jnp.where(polar, on, second_b), True)

    queries, *state = attend(
        heads, (0, 1, 3, 4, 5), lists, head_scale, [second, second_a, on, on_a, on_b],
        [w_key, w_value, w_query], None, None,
    )
    off, queries = lax.optimization_barrier((off, queries))
    on_y = across(off, False)
    (result,) = attend(
        heads, (6, 7, 8, 9), lists, head_scale, [off, off_a, third, on_y, second_b], [w_key, w_value],
        [queries, *state], [w_out, hidden],
    )
    return result.reshape(rows, cols, model)


def solution(mesh):
    return jax.shard_map(
        on_device,
        mesh=mesh,
        in_specs=(
            P("lat", "lon", None),
            P(),
            P(),
            P(),
            P(),
            P(),
            P(),
            P(),
            P(),
            P("lat", "lon", None),
        ),
        out_specs=P("lat", "lon", None),
        check_vma=False,
    )
```

```python
import functools
import math

import jax
import jax.numpy as jnp
from jax import lax
from jax.experimental import pallas as pl
from jax.experimental.pallas import tpu as pltpu
from jax.sharding import PartitionSpec as P

EPS = 1e-06
BIG = 1e30
VMEM = pl.BlockSpec(memory_space=pltpu.VMEM)
SMEM = pl.BlockSpec(memory_space=pltpu.SMEM)


def pair_swaps(count, first):
    pairs = []
    for low in range(first, count - 1, 2):
        pairs += [(low, low + 1), (low + 1, low)]
    return pairs


def lon_pairs(lats, lat_count, lon_count, off_chip):
    pairs = []
    for lat in lats:
        for low in range(1 if off_chip else 0, lon_count, 2):
            one, two = lat * lon_count + low, lat * lon_count + (low + 1) % lon_count
            pairs += [(one, two), (two, one)]
    return pairs


def two_away(count, first):
    pairs = []
    for start in range(first, count, 4):
        for low in (start, start + 1):
            if low + 2 < count:
                pairs += [(low, low + 2), (low + 2, low)]
    return pairs


def permuted(value, axis, pairs):
    if not pairs:
        return jnp.zeros_like(value)
    return lax.ppermute(value, axis, pairs)


def unit(values):
    return lax.rsqrt(jnp.mean(values * values, axis=-1, keepdims=True) + EPS)


def partner(place, count, off_chip):
    even = place % 2 == 0
    if not off_chip:
        return jnp.where(even, place + 1, place - 1)
    return jnp.where(even, jnp.where(place == 0, count - 1, place - 1), jnp.where(place == count - 1, 0, place + 1))


def band_facts():
    lats = lax.axis_size("lat")
    band = lax.axis_index("lat")
    even = band % 2 == 0
    polar = (band == 0) | (band == lats - 1)
    return band, jnp.where(even, band + 1, band - 1), jnp.where(even, band - 1, band + 1), polar


def slot_penalties(pattern, slots):
    lons = lax.axis_size("lon")
    band, band_a, band_b, polar = band_facts()
    sector = lax.axis_index("lon")
    on, off = partner(sector, lons, False), partner(sector, lons, True)
    places = [
        (band, sector), (band_a, sector), (band_b, sector),
        (band, on), (band_a, on), (band_b, on),
        (band, off), (band_a, off),
        (jnp.where(polar, band, band_b), jnp.where(polar, partner(off, lons, False), off)),
        (jnp.where(polar, band, band_b), jnp.where(polar, partner(on, lons, True), sector)),
    ]
    exists = {2: ~polar, 5: ~polar}
    out = []
    for slot in slots:
        tile = places[slot][0] * lons + places[slot][1]
        listed = pattern[0] == tile
        for index in range(1, pattern.shape[0]):
            listed = listed | (pattern[index] == tile)
        if slot in exists:
            listed = listed & exists[slot]
        out.append(jnp.where(listed, 0.0, BIG).astype(jnp.float32))
    return out


def prep_kernel(tok, tok_out, edges, brink):
    rows, cols, width = tok.shape
    tok_out[...] = tok[...]
    first = lax.broadcasted_iota(jnp.int32, (2 * rows, width), 0)
    out = jnp.zeros((2 * rows, width), jnp.float32)
    for row in range(rows):
        line = tok[row].astype(jnp.float32)
        out = jnp.where(first == row, line[0:1], out)
        out = jnp.where(first == rows + row, line[cols - 1 : cols], out)
    edges[...] = out.astype(edges.dtype)
    brink[:cols, :] = tok[0]
    brink[cols:, :] = tok[rows - 1]


def conv_kernel(
    tok, tile_a, tile_b, halo, halo_a, halo_b, ring_a, ring_b, gains,
    hidden, second, second_a, second_b, copy_b, before, middle, after, mixed,
):
    rows, cols, width = tok.shape
    gain_one, gain_two = gains[0:1, :], gains[1:2, :]
    place = lax.broadcasted_iota(jnp.int32, (cols, width), 0)

    def normed(raw):
        wide = raw.astype(jnp.float32)
        return (wide * unit(wide) * gain_one).astype(jnp.bfloat16).astype(jnp.float32)

    def put(row, value, left, right):
        middle[row] = value
        before[row] = jnp.where(place == 0, left, pltpu.roll(value, 1, 0))
        after[row] = jnp.where(place == cols - 1, right, pltpu.roll(value, cols - 1, 0))

    def tile_rows(base, raw, edges):
        sides = normed(edges[...])
        for row in range(rows):
            put(base + row, normed(raw[row]), sides[row : row + 1], sides[rows + row : rows + row + 1])

    def ring(row, data, bottom):
        base = pl.multiple_of(bottom * cols, cols)
        sides = normed(data[2 * cols :, :])
        left = jnp.where(bottom > 0, sides[rows - 1 : rows], sides[0:1])
        right = jnp.where(bottom > 0, sides[2 * rows - 1 : 2 * rows], sides[rows : rows + 1])
        put(row, normed(data[pl.ds(base, cols), :]), left, right)

    band = lax.axis_index("lat")
    odd = band % 2
    high = (band // 2) % 2
    base_own = 1 + rows
    base_a = jnp.where(odd > 0, 1, 1 + 2 * rows)
    base_b = jnp.where(odd > 0, 1 + 2 * rows, 1)
    last_row = 1 + 3 * rows
    tile_rows(base_own, tok, halo)
    tile_rows(base_a, tile_a, halo_a)
    tile_rows(base_b, tile_b, halo_b)
    ring(jnp.where(high > 0, 0, last_row), ring_a, high)
    ring(jnp.where(high > 0, last_row, 0), ring_b, 1 - high)

    for base, raw, out, keep in (
        (base_own, tok, second, True), (base_a, tile_a, second_a, False), (base_b, tile_b, second_b, False),
    ):
        for start in range(0, width, 256):
            lanes = slice(start, start + 256)
            taps = [gains[2 + index : 3 + index, lanes] for index in range(9)]
            totals = [None] * rows
            for row in range(-1, rows + 1):
                parts = [ref[base + row, :, lanes] for ref in (before, middle, after)]
                for target in range(max(row - 1, 0), min(row + 2, rows)):
                    for along in range(3):
                        term = parts[along] * taps[3 * (row - target + 1) + along]
                        totals[target] = term if totals[target] is None else totals[target] + term
            for row in range(rows):
                mixed[row * cols : (row + 1) * cols, lanes] = (
                    raw[row, :, lanes].astype(jnp.float32) + totals[row]
                ).astype(jnp.bfloat16)
        if keep:
            hidden[...] = mixed[...]
        for row in range(rows):
            at = slice(row * cols, (row + 1) * cols)
            wide = mixed[at, :].astype(jnp.float32)
            out[at, :] = (wide * unit(wide) * gain_two).astype(jnp.bfloat16)
    copy_b[...] = second_b[...]


def head_marks(model, head):
    channel = lax.broadcasted_iota(jnp.int32, (model, 128), 0) // head
    index = lax.broadcasted_iota(jnp.int32, (model, 128), 1) % 64
    return jnp.where(channel == index, 1.0, 0.0).astype(jnp.bfloat16)


def head_units(wide, marks, head):
    square = (wide * wide).astype(jnp.bfloat16)
    total = jnp.dot(square, marks, preferred_element_type=jnp.float32)
    share = lax.rsqrt(total * (1.0 / head) + EPS)
    high = share.astype(jnp.bfloat16).astype(jnp.float32)
    lane = lax.broadcasted_iota(jnp.int32, share.shape, 1)
    split = jnp.where(lane < 64, high, share - high).astype(jnp.bfloat16)
    factor = lax.dot_general(
        split, marks, (((1,), (1,)), ((), ())), preferred_element_type=jnp.float32
    )
    return (wide * factor).astype(jnp.bfloat16)


CHUNK = 256


def group_kernel(heads, slots, first, last, *refs):
    refs = list(refs)

    def take(count):
        out = refs[:count]
        del refs[:count]
        return out

    pattern, scale_in = take(2)
    tiles = take(len(slots) + last)
    w_key, w_value = take(2)
    if first:
        (w_query,) = take(1)
    else:
        queries, tops, lows, sums = take(4)
    if last:
        w_out, hidden, result = take(3)
    else:
        if first:
            (queries,) = take(1)
        tops_out, lows_out, sums_out = take(3)
    keys, values = take(2)
    if last:
        (joined,) = take(1)

    size, model = tiles[0].shape
    head = model // heads
    width = 2 * head
    marks = head_marks(model, head)
    if first:
        raw_query = jnp.dot(tiles[0][...], w_query[...], preferred_element_type=jnp.float32)
    tokens = [ref[...] for ref in tiles]
    if last:
        other = tokens.pop()
        tokens[-1] = jnp.where(band_facts()[3], tokens[-1], other)
    tokens = jnp.concatenate(tokens, axis=0)
    held = None
    for start in range(0, model, CHUNK):
        part = slice(start, start + CHUNK)
        raw = jnp.dot(tokens, w_key[:, part], preferred_element_type=jnp.float32)
        if held is not None:
            keys[:, held[0]] = head_units(held[1], marks[:CHUNK], head)
        elif first:
            queries[...] = head_units(raw_query, marks, head)
        held = (part, raw)
    values[...] = lax.dot_general(
        w_value[...], tokens, (((1,), (1,)), ((), ())), preferred_element_type=jnp.float32
    ).astype(jnp.bfloat16)
    keys[:, held[0]] = head_units(held[1], marks[:CHUNK], head)

    flags = slot_penalties(pattern, slots)
    factor = math.log2(math.e) / math.sqrt(head)
    lane = lax.broadcasted_iota(jnp.int32, (size, width), 1)
    half = lax.broadcasted_iota(jnp.int32, (1, 2 * size), 1) < size
    def weigh(pair):
        lanes = slice(pair * width, (pair + 1) * width)
        query = queries[:, lanes]
        zero = jnp.zeros_like(query)
        both = jnp.concatenate(
            [jnp.where(lane < head, query, zero), jnp.where(lane < head, zero, query)], axis=0
        )
        scores = lax.dot_general(
            keys[:, lanes], both, (((1,), (1,)), ((), ())), preferred_element_type=jnp.float32
        )
        scale = jnp.where(half, scale_in[2 * pair] * factor, scale_in[2 * pair + 1] * factor)
        parts = [scores[slot * size : (slot + 1) * size] * scale for slot in range(len(slots))]
        best = None if first else tops[pair : pair + 1, :]
        for part, flag in zip(parts, flags):
            peak = jnp.max(part, axis=0, keepdims=True) - flag
            best = peak if best is None else jnp.maximum(best, peak)
        exps = [jnp.exp2(part - (best + flag)) for part, flag in zip(parts, flags)]
        total = exps[0]
        for part in exps[1:]:
            total = total + part
        low = jnp.sum(total, axis=0, keepdims=True)
        return best, low, jnp.concatenate([part.astype(jnp.bfloat16) for part in exps], axis=0)

    def mix(pair, best, low, weights):
        lanes = slice(pair * width, (pair + 1) * width)
        mixed = jnp.dot(values[lanes, :], weights, preferred_element_type=jnp.float32)
        mixed = jnp.concatenate([mixed[:head, :size], mixed[head:, size:]], axis=0)
        if not first:
            old = jnp.exp2(tops[pair : pair + 1, :] - best)
            low = low + old * lows[pair : pair + 1, :]
            mixed = mixed + sums[lanes, :] * spans(old, size, head)
        if last:
            joined[:, lanes] = jnp.transpose(mixed * spans(1.0 / low, size, head)).astype(jnp.bfloat16)
        else:
            sums_out[lanes, :] = mixed
            tops_out[pair : pair + 1, :] = best
            lows_out[pair : pair + 1, :] = low

    waiting = []
    for pair in range(heads // 2):
        waiting.append((pair, *weigh(pair)))
        if len(waiting) > 3:
            mix(*waiting.pop(0))
    for entry in waiting:
        mix(*entry)
    if not last:
        return
    attended = joined[...]
    for start in range(0, model, CHUNK):
        part = slice(start, start + CHUNK)
        out = jnp.dot(attended, w_out[:, part], preferred_element_type=jnp.float32)
        result[:, part] = (hidden[:, part].astype(jnp.float32) + out).astype(jnp.bfloat16)


def spans(row, size, head):
    return jnp.concatenate(
        [jnp.broadcast_to(row[:, :size], (head, size)), jnp.broadcast_to(row[:, size:], (head, size))],
        axis=0,
    )


def limit(mebibytes):
    return pltpu.CompilerParams(vmem_limit_bytes=mebibytes * 2**20)


def attend(heads, slots, pattern, scale, tiles, weights, state, finish):
    first, last = state is None, finish is not None
    size, model = tiles[0].shape
    tile = jax.ShapeDtypeStruct((size, model), jnp.bfloat16)
    stats = jax.ShapeDtypeStruct((heads // 2, 2 * size), jnp.float32)
    out = [stats, stats, jax.ShapeDtypeStruct((model, size), jnp.float32)]
    if last:
        out = [tile]
    elif first:
        out = [tile] + out
    operands = [pattern, scale, *tiles, *weights]
    if not first:
        operands += list(state)
    if last:
        operands += list(finish)
    scratch = [
        pltpu.VMEM((len(slots) * size, model), jnp.bfloat16),
        pltpu.VMEM((model, len(slots) * size), jnp.bfloat16),
    ]
    if last:
        scratch.append(pltpu.VMEM((size, model), jnp.bfloat16))
    return pl.pallas_call(
        functools.partial(group_kernel, heads, slots, first, last),
        out_shape=out,
        in_specs=[SMEM, SMEM] + [VMEM] * (len(operands) - 2),
        out_specs=[VMEM] * len(out),
        scratch_shapes=scratch,
        compiler_params=limit(16),
        cost_estimate=pl.CostEstimate(
            flops=2**36, bytes_accessed=2**28, transcendentals=0
        ),
        name="attend" + "_".join(str(slot) for slot in slots),
    )(*operands)


def on_device(
    tokens, norm1_gain, conv_weight, norm2_gain, w_query, w_key, w_value, w_out, head_scale, pattern
):
    rows, cols, model = tokens.shape
    size = rows * cols
    heads = head_scale.shape[0]
    lats, lons = lax.axis_size("lat"), lax.axis_size("lon")
    polar = band_facts()[3]
    even_sector = lax.axis_index("lon") % 2 == 0
    lists = pattern.reshape(-1)

    swap_a = functools.partial(permuted, axis="lat", pairs=pair_swaps(lats, 0))
    swap_b = functools.partial(permuted, axis="lat", pairs=pair_swaps(lats, 1))

    def across(value, off_chip):
        return permuted(value, ("lat", "lon"), lon_pairs(range(lats), lats, lons, off_chip))

    tile_a, tile_b = swap_a(tokens), swap_b(tokens)
    tok, edges, brink = pl.pallas_call(
        prep_kernel,
        out_shape=[
            jax.ShapeDtypeStruct(shape, tokens.dtype)
            for shape in (tokens.shape, (2 * rows, model), (2 * cols, model))
        ],
        in_specs=[VMEM],
        out_specs=[VMEM] * 3,
        compiler_params=limit(2),
        cost_estimate=pl.CostEstimate(flops=0, bytes_accessed=2**21, transcendentals=0),
        name="prep",
    )(tokens)
    gains = jnp.concatenate(
        [norm1_gain.reshape(1, model), norm2_gain.reshape(1, model), conv_weight.reshape(9, model)],
        axis=0,
    )
    on_edges, off_edges = across(edges, False), across(edges, True)
    halo = jnp.concatenate(
        [
            jnp.where(even_sector, off_edges[rows:], on_edges[rows:]),
            jnp.where(even_sector, on_edges[:rows], off_edges[:rows]),
        ],
        axis=0,
    )
    halo_a, halo_b = swap_a(halo), swap_b(halo)
    brink = jnp.concatenate([brink, halo], axis=0)
    ring_a = permuted(brink, "lat", two_away(lats, 0))
    ring_b = permuted(brink, "lat", two_away(lats, 2))

    tile = jax.ShapeDtypeStruct((size, model), jnp.bfloat16)
    w_value = jnp.transpose(w_value)
    gains, w_value = lax.optimization_barrier((gains, w_value))
    window = pltpu.VMEM((2 + 3 * rows, cols, model), jnp.float32)
    hidden, second, second_a, second_b, copy_b = pl.pallas_call(
        conv_kernel,
        out_shape=[tile] * 5,
        in_specs=[VMEM] * 9,
        out_specs=[VMEM] * 5,
        scratch_shapes=[window] * 3 + [pltpu.VMEM((size, model), jnp.bfloat16)],
        compiler_params=limit(10),
        cost_estimate=pl.CostEstimate(flops=2**24, bytes_accessed=24 * 2**20, transcendentals=0),
        name="conv",
    )(
        tok, tile_a, tile_b, halo, halo_a, halo_b, ring_a, ring_b, gains
    )

    on = across(second, False)
    off = across(second, True)
    on_a, on_b = across(second_a, False), across(copy_b, False)
    off_a = across(second_a, True)
    third = across(jnp.where(polar, on, second_b), True)

    queries, *state = attend(
        heads, (0, 1, 3, 4, 5), lists, head_scale, [second, second_a, on, on_a, on_b],
        [w_key, w_value, w_query], None, None,
    )
    off, queries = lax.optimization_barrier((off, queries))
    on_y = across(off, False)
    (result,) = attend(
        heads, (6, 7, 8, 9), lists, head_scale, [off, off_a, third, on_y, second_b], [w_key, w_value],
        [queries, *state], [w_out, hidden],
    )
    return result.reshape(rows, cols, model)


def solution(mesh):
    return jax.shard_map(
        on_device,
        mesh=mesh,
        in_specs=(
            P("lat", "lon", None),
            P(),
            P(),
            P(),
            P(),
            P(),
            P(),
            P(),
            P(),
            P("lat", "lon", None),
        ),
        out_specs=P("lat", "lon", None),
        check_vma=False,
    )
```

```python
import functools
import math

import jax
import jax.numpy as jnp
from jax import lax
from jax.experimental import pallas as pl
from jax.experimental.pallas import tpu as pltpu
from jax.sharding import PartitionSpec as P

EPS = 1e-06
BIG = 1e30
VMEM = pl.BlockSpec(memory_space=pltpu.VMEM)
SMEM = pl.BlockSpec(memory_space=pltpu.SMEM)


def pair_swaps(count, first):
    pairs = []
    for low in range(first, count - 1, 2):
        pairs += [(low, low + 1), (low + 1, low)]
    return pairs


def lon_pairs(lats, lat_count, lon_count, off_chip):
    pairs = []
    for lat in lats:
        for low in range(1 if off_chip else 0, lon_count, 2):
            one, two = lat * lon_count + low, lat * lon_count + (low + 1) % lon_count
            pairs += [(one, two), (two, one)]
    return pairs


def two_away(count, first):
    pairs = []
    for start in range(first, count, 4):
        for low in (start, start + 1):
            if low + 2 < count:
                pairs += [(low, low + 2), (low + 2, low)]
    return pairs


def permuted(value, axis, pairs):
    if not pairs:
        return jnp.zeros_like(value)
    return lax.ppermute(value, axis, pairs)


def unit(values):
    return lax.rsqrt(jnp.mean(values * values, axis=-1, keepdims=True) + EPS)


def partner(place, count, off_chip):
    even = place % 2 == 0
    if not off_chip:
        return jnp.where(even, place + 1, place - 1)
    return jnp.where(even, jnp.where(place == 0, count - 1, place - 1), jnp.where(place == count - 1, 0, place + 1))


def band_facts():
    lats = lax.axis_size("lat")
    band = lax.axis_index("lat")
    even = band % 2 == 0
    polar = (band == 0) | (band == lats - 1)
    return band, jnp.where(even, band + 1, band - 1), jnp.where(even, band - 1, band + 1), polar


def slot_penalties(pattern, slots):
    lons = lax.axis_size("lon")
    band, band_a, band_b, polar = band_facts()
    sector = lax.axis_index("lon")
    on, off = partner(sector, lons, False), partner(sector, lons, True)
    places = [
        (band, sector), (band_a, sector), (band_b, sector),
        (band, on), (band_a, on), (band_b, on),
        (band, off), (band_a, off),
        (jnp.where(polar, band, band_b), jnp.where(polar, partner(off, lons, False), off)),
        (jnp.where(polar, band, band_b), jnp.where(polar, partner(on, lons, True), sector)),
    ]
    exists = {2: ~polar, 5: ~polar}
    out = []
    for slot in slots:
        tile = places[slot][0] * lons + places[slot][1]
        listed = pattern[0] == tile
        for index in range(1, pattern.shape[0]):
            listed = listed | (pattern[index] == tile)
        if slot in exists:
            listed = listed & exists[slot]
        out.append(jnp.where(listed, 0.0, BIG).astype(jnp.float32))
    return out


def prep_kernel(tok, tok_out, edges, brink):
    rows, cols, width = tok.shape
    tok_out[...] = tok[...]
    first = lax.broadcasted_iota(jnp.int32, (2 * rows, width), 0)
    out = jnp.zeros((2 * rows, width), jnp.float32)
    for row in range(rows):
        line = tok[row].astype(jnp.float32)
        out = jnp.where(first == row, line[0:1], out)
        out = jnp.where(first == rows + row, line[cols - 1 : cols], out)
    edges[...] = out.astype(edges.dtype)
    brink[:cols, :] = tok[0]
    brink[cols:, :] = tok[rows - 1]


def conv_kernel(
    tok, tile_a, tile_b, halo, halo_a, halo_b, ring_a, ring_b, gains,
    hidden, second, second_a, second_b, copy_b, before, middle, after, mixed,
):
    rows, cols, width = tok.shape
    gain_one, gain_two = gains[0:1, :], gains[1:2, :]
    place = lax.broadcasted_iota(jnp.int32, (cols, width), 0)

    def normed(raw):
        wide = raw.astype(jnp.float32)
        return (wide * unit(wide) * gain_one).astype(jnp.bfloat16).astype(jnp.float32)

    def put(row, value, left, right):
        middle[row] = value
        before[row] = jnp.where(place == 0, left, pltpu.roll(value, 1, 0))
        after[row] = jnp.where(place == cols - 1, right, pltpu.roll(value, cols - 1, 0))

    def tile_rows(base, raw, edges):
        sides = normed(edges[...])
        for row in range(rows):
            put(base + row, normed(raw[row]), sides[row : row + 1], sides[rows + row : rows + row + 1])

    def ring(row, data, bottom):
        base = pl.multiple_of(bottom * cols, cols)
        sides = normed(data[2 * cols :, :])
        left = jnp.where(bottom > 0, sides[rows - 1 : rows], sides[0:1])
        right = jnp.where(bottom > 0, sides[2 * rows - 1 : 2 * rows], sides[rows : rows + 1])
        put(row, normed(data[pl.ds(base, cols), :]), left, right)

    band = lax.axis_index("lat")
    odd = band % 2
    high = (band // 2) % 2
    base_own = 1 + rows
    base_a = jnp.where(odd > 0, 1, 1 + 2 * rows)
    base_b = jnp.where(odd > 0, 1 + 2 * rows, 1)
    last_row = 1 + 3 * rows
    tile_rows(base_own, tok, halo)
    tile_rows(base_a, tile_a, halo_a)
    tile_rows(base_b, tile_b, halo_b)
    ring(jnp.where(high > 0, 0, last_row), ring_a, high)
    ring(jnp.where(high > 0, last_row, 0), ring_b, 1 - high)

    for base, raw, out, keep in (
        (base_own, tok, second, True), (base_a, tile_a, second_a, False), (base_b, tile_b, second_b, False),
    ):
        for start in range(0, width, 256):
            lanes = slice(start, start + 256)
            taps = [gains[2 + index : 3 + index, lanes] for index in range(9)]
            totals = [None] * rows
            for row in range(-1, rows + 1):
                parts = [ref[base + row, :, lanes] for ref in (before, middle, after)]
                for target in range(max(row - 1, 0), min(row + 2, rows)):
                    for along in range(3):
                        term = parts[along] * taps[3 * (row - target + 1) + along]
                        totals[target] = term if totals[target] is None else totals[target] + term
            for row in range(rows):
                mixed[row * cols : (row + 1) * cols, lanes] = (
                    raw[row, :, lanes].astype(jnp.float32) + totals[row]
                ).astype(jnp.bfloat16)
        if keep:
            hidden[...] = mixed[...]
        for row in range(rows):
            at = slice(row * cols, (row + 1) * cols)
            wide = mixed[at, :].astype(jnp.float32)
            out[at, :] = (wide * unit(wide) * gain_two).astype(jnp.bfloat16)
    copy_b[...] = second_b[...]


def head_marks(model, head):
    channel = lax.broadcasted_iota(jnp.int32, (model, 128), 0) // head
    index = lax.broadcasted_iota(jnp.int32, (model, 128), 1) % 64
    return jnp.where(channel == index, 1.0, 0.0).astype(jnp.bfloat16)


def head_units(wide, marks, head):
    square = (wide * wide).astype(jnp.bfloat16)
    total = jnp.dot(square, marks, preferred_element_type=jnp.float32)
    share = lax.rsqrt(total * (1.0 / head) + EPS)
    high = share.astype(jnp.bfloat16).astype(jnp.float32)
    lane = lax.broadcasted_iota(jnp.int32, share.shape, 1)
    split = jnp.where(lane < 64, high, share - high).astype(jnp.bfloat16)
    factor = lax.dot_general(
        split, marks, (((1,), (1,)), ((), ())), preferred_element_type=jnp.float32
    )
    return (wide * factor).astype(jnp.bfloat16)


CHUNK = 256


def group_kernel(heads, slots, first, last, *refs):
    refs = list(refs)

    def take(count):
        out = refs[:count]
        del refs[:count]
        return out

    pattern, scale_in = take(2)
    tiles = take(len(slots) + last)
    w_key, w_value = take(2)
    if first:
        (w_query,) = take(1)
    else:
        queries, tops, lows, sums = take(4)
    if last:
        w_out, hidden, result = take(3)
    else:
        if first:
            (queries,) = take(1)
        tops_out, lows_out, sums_out = take(3)
    keys, values = take(2)
    if last:
        (joined,) = take(1)

    size, model = tiles[0].shape
    head = model // heads
    width = 2 * head
    marks = head_marks(model, head)
    if first:
        raw_query = jnp.dot(tiles[0][...], w_query[...], preferred_element_type=jnp.float32)
    tokens = [ref[...] for ref in tiles]
    if last:
        other = tokens.pop()
        tokens[-1] = jnp.where(band_facts()[3], tokens[-1], other)
    tokens = jnp.concatenate(tokens, axis=0)
    held = None
    for start in range(0, model, CHUNK):
        part = slice(start, start + CHUNK)
        raw = jnp.dot(tokens, w_key[:, part], preferred_element_type=jnp.float32)
        if held is not None:
            keys[:, held[0]] = head_units(held[1], marks[:CHUNK], head)
        elif first:
            queries[...] = head_units(raw_query, marks, head)
        held = (part, raw)
    values[...] = lax.dot_general(
        w_value[...], tokens, (((1,), (1,)), ((), ())), preferred_element_type=jnp.float32
    ).astype(jnp.bfloat16)
    keys[:, held[0]] = head_units(held[1], marks[:CHUNK], head)

    flags = slot_penalties(pattern, slots)
    factor = math.log2(math.e) / math.sqrt(head)
    lane = lax.broadcasted_iota(jnp.int32, (size, width), 1)
    half = lax.broadcasted_iota(jnp.int32, (1, 2 * size), 1) < size
    def weigh(pair):
        lanes = slice(pair * width, (pair + 1) * width)
        query = queries[:, lanes]
        zero = jnp.zeros_like(query)
        both = jnp.concatenate(
            [jnp.where(lane < head, query, zero), jnp.where(lane < head, zero, query)], axis=0
        )
        scores = lax.dot_general(
            keys[:, lanes], both, (((1,), (1,)), ((), ())), preferred_element_type=jnp.float32
        )
        scale = jnp.where(half, scale_in[2 * pair] * factor, scale_in[2 * pair + 1] * factor)
        parts = [scores[slot * size : (slot + 1) * size] * scale for slot in range(len(slots))]
        best = None if first else tops[pair : pair + 1, :]
        for part, flag in zip(parts, flags):
            peak = jnp.max(part, axis=0, keepdims=True) - flag
            best = peak if best is None else jnp.maximum(best, peak)
        exps = [jnp.exp2(part - (best + flag)) for part, flag in zip(parts, flags)]
        total = exps[0]
        for part in exps[1:]:
            total = total + part
        low = jnp.sum(total, axis=0, keepdims=True)
        return best, low, jnp.concatenate([part.astype(jnp.bfloat16) for part in exps], axis=0)

    def mix(pair, best, low, weights):
        lanes = slice(pair * width, (pair + 1) * width)
        mixed = jnp.dot(values[lanes, :], weights, preferred_element_type=jnp.float32)
        mixed = jnp.concatenate([mixed[:head, :size], mixed[head:, size:]], axis=0)
        if not first:
            old = jnp.exp2(tops[pair : pair + 1, :] - best)
            low = low + old * lows[pair : pair + 1, :]
            mixed = mixed + sums[lanes, :] * spans(old, size, head)
        if last:
            joined[:, lanes] = jnp.transpose(mixed * spans(1.0 / low, size, head)).astype(jnp.bfloat16)
        else:
            sums_out[lanes, :] = mixed
            tops_out[pair : pair + 1, :] = best
            lows_out[pair : pair + 1, :] = low

    waiting = []
    for pair in range(heads // 2):
        waiting.append((pair, *weigh(pair)))
        if len(waiting) > 4:
            mix(*waiting.pop(0))
    for entry in waiting:
        mix(*entry)
    if not last:
        return
    attended = joined[...]
    for start in range(0, model, CHUNK):
        part = slice(start, start + CHUNK)
        out = jnp.dot(attended, w_out[:, part], preferred_element_type=jnp.float32)
        result[:, part] = (hidden[:, part].astype(jnp.float32) + out).astype(jnp.bfloat16)


def spans(row, size, head):
    return jnp.concatenate(
        [jnp.broadcast_to(row[:, :size], (head, size)), jnp.broadcast_to(row[:, size:], (head, size))],
        axis=0,
    )


def limit(mebibytes):
    return pltpu.CompilerParams(vmem_limit_bytes=mebibytes * 2**20)


def attend(heads, slots, pattern, scale, tiles, weights, state, finish):
    first, last = state is None, finish is not None
    size, model = tiles[0].shape
    tile = jax.ShapeDtypeStruct((size, model), jnp.bfloat16)
    stats = jax.ShapeDtypeStruct((heads // 2, 2 * size), jnp.float32)
    out = [stats, stats, jax.ShapeDtypeStruct((model, size), jnp.float32)]
    if last:
        out = [tile]
    elif first:
        out = [tile] + out
    operands = [pattern, scale, *tiles, *weights]
    if not first:
        operands += list(state)
    if last:
        operands += list(finish)
    scratch = [
        pltpu.VMEM((len(slots) * size, model), jnp.bfloat16),
        pltpu.VMEM((model, len(slots) * size), jnp.bfloat16),
    ]
    if last:
        scratch.append(pltpu.VMEM((size, model), jnp.bfloat16))
    return pl.pallas_call(
        functools.partial(group_kernel, heads, slots, first, last),
        out_shape=out,
        in_specs=[SMEM, SMEM] + [VMEM] * (len(operands) - 2),
        out_specs=[VMEM] * len(out),
        scratch_shapes=scratch,
        compiler_params=limit(16),
        cost_estimate=pl.CostEstimate(
            flops=2**36, bytes_accessed=2**28, transcendentals=0
        ),
        name="attend" + "_".join(str(slot) for slot in slots),
    )(*operands)


def on_device(
    tokens, norm1_gain, conv_weight, norm2_gain, w_query, w_key, w_value, w_out, head_scale, pattern
):
    rows, cols, model = tokens.shape
    size = rows * cols
    heads = head_scale.shape[0]
    lats, lons = lax.axis_size("lat"), lax.axis_size("lon")
    polar = band_facts()[3]
    even_sector = lax.axis_index("lon") % 2 == 0
    lists = pattern.reshape(-1)

    swap_a = functools.partial(permuted, axis="lat", pairs=pair_swaps(lats, 0))
    swap_b = functools.partial(permuted, axis="lat", pairs=pair_swaps(lats, 1))

    def across(value, off_chip):
        return permuted(value, ("lat", "lon"), lon_pairs(range(lats), lats, lons, off_chip))

    tile_a, tile_b = swap_a(tokens), swap_b(tokens)
    tok, edges, brink = pl.pallas_call(
        prep_kernel,
        out_shape=[
            jax.ShapeDtypeStruct(shape, tokens.dtype)
            for shape in (tokens.shape, (2 * rows, model), (2 * cols, model))
        ],
        in_specs=[VMEM],
        out_specs=[VMEM] * 3,
        compiler_params=limit(2),
        cost_estimate=pl.CostEstimate(flops=0, bytes_accessed=2**21, transcendentals=0),
        name="prep",
    )(tokens)
    gains = jnp.concatenate(
        [norm1_gain.reshape(1, model), norm2_gain.reshape(1, model), conv_weight.reshape(9, model)],
        axis=0,
    )
    on_edges, off_edges = across(edges, False), across(edges, True)
    halo = jnp.concatenate(
        [
            jnp.where(even_sector, off_edges[rows:], on_edges[rows:]),
            jnp.where(even_sector, on_edges[:rows], off_edges[:rows]),
        ],
        axis=0,
    )
    halo_a, halo_b = swap_a(halo), swap_b(halo)
    brink = jnp.concatenate([brink, halo], axis=0)
    ring_a = permuted(brink, "lat", two_away(lats, 0))
    ring_b = permuted(brink, "lat", two_away(lats, 2))

    tile = jax.ShapeDtypeStruct((size, model), jnp.bfloat16)
    w_value = jnp.transpose(w_value)
    gains, w_value = lax.optimization_barrier((gains, w_value))
    window = pltpu.VMEM((2 + 3 * rows, cols, model), jnp.float32)
    hidden, second, second_a, second_b, copy_b = pl.pallas_call(
        conv_kernel,
        out_shape=[tile] * 5,
        in_specs=[VMEM] * 9,
        out_specs=[VMEM] * 5,
        scratch_shapes=[window] * 3 + [pltpu.VMEM((size, model), jnp.bfloat16)],
        compiler_params=limit(10),
        cost_estimate=pl.CostEstimate(flops=2**24, bytes_accessed=24 * 2**20, transcendentals=0),
        name="conv",
    )(
        tok, tile_a, tile_b, halo, halo_a, halo_b, ring_a, ring_b, gains
    )

    on = across(second, False)
    off = across(second, True)
    on_a, on_b = across(second_a, False), across(copy_b, False)
    off_a = across(second_a, True)
    third = across(jnp.where(polar, on, second_b), True)

    queries, *state = attend(
        heads, (0, 1, 3, 4, 5), lists, head_scale, [second, second_a, on, on_a, on_b],
        [w_key, w_value, w_query], None, None,
    )
    off, queries = lax.optimization_barrier((off, queries))
    on_y = across(off, False)
    (result,) = attend(
        heads, (6, 7, 8, 9), lists, head_scale, [off, off_a, third, on_y, second_b], [w_key, w_value],
        [queries, *state], [w_out, hidden],
    )
    return result.reshape(rows, cols, model)


def solution(mesh):
    return jax.shard_map(
        on_device,
        mesh=mesh,
        in_specs=(
            P("lat", "lon", None),
            P(),
            P(),
            P(),
            P(),
            P(),
            P(),
            P(),
            P(),
            P("lat", "lon", None),
        ),
        out_specs=P("lat", "lon", None),
        check_vma=False,
    )
```
